512 devices in a mesh: seq: 64 (over y, z), fsdp: 8 (over x, core).
Axes of the slice: x: 4, y: 4, z: 16, core: 2. Of those that a mesh axis runs over, the one named last changes fastest.
Arguments:
- probe_tensor: bfloat16 [8192, 8, 2048], P('seq', 'fsdp'), may hold values from -10 to 10
- matcher_tensor: bfloat16 [8192, 8, 2048], P('seq', 'fsdp'), may hold values from -10 to 10
- payload_tensor: bfloat16 [8192, 8, 2048], P('seq', 'fsdp'), may hold values from -6 to 6
- adjoint_attended: bfloat16 [8192, 8, 2048], P('seq', 'fsdp'), may hold values from -6 to 6
- logit_scale: float32 [16], replicated, may hold values from 0.5 to 2
- anchor_tiles: int32 [16, 2], replicated, may hold values from 0 to 127, as said below
- sampled_tiles: int32 [16, 128, 3], replicated, may hold values from 0 to 127, as said below
Outputs:
- query_gradients: bfloat16 [8192, 8, 2048], P('seq', 'fsdp')
- grad_key: bfloat16 [8192, 8, 2048], P('seq', 'fsdp')
- grad_value: bfloat16 [8192, 8, 2048], P('seq', 'fsdp')
- adjoint_scales: float32 [16], replicated
The draws below stay inside these ranges and needn't reach their ends.
Inputs may be any that keep to these rules, and one draw needn't show every extreme that they name: `anchor_tiles`: each head lists 2 different blocks. `sampled_tiles`: each row lists 3 different blocks, none within one block of the row's own block and none among the head's global blocks.
All inputs are finite; a program needn't handle non-finite values.
Results may differ from the reference program's by a relative error of at most 0.0083.
Values may be sent and summed in bfloat16 or wider, within the bound.
No kernel may reach another device: no remote copies, remote signals or barrier semaphores. Data moves between devices by JAX's collectives and lax.ppermute only.
A program may use at most 64 MiB of HBM per device.

```python
import math
import jax
import jax.numpy as jnp
from jax import lax

CHANNEL_TOTAL = 16
HEAD_DIM = 128
TILE_SPAN = 64
GLOBALS = 2
RANDOM = 3
SEQ_TOK = 128
ATT_WIDTH = 2048
BATCH = 8
LENGTH = 8192
SHARES = 4
N_SEQ = 64


def drawn_pair(key):
    full_shape = (LENGTH, BATCH, CHANNEL_TOTAL * HEAD_DIM)
    drawn_query = jnp.clip(jax.random.normal(jax.random.fold_in(key, 101), full_shape, jnp.float32), -6.0, 6.0)
    drawn_key = jnp.clip(jax.random.normal(jax.random.fold_in(key, 102), full_shape, jnp.float32), -6.0, 6.0)
    return (drawn_query, drawn_key)


def draw_probe_tensor(key, part):
    return drawn_pair(key)[0].astype(jnp.bfloat16)


def draw_matcher_tensor(key, part):
    return drawn_pair(key)[1].astype(jnp.bfloat16)


def pick_globals(key):
    nblocks = LENGTH // TILE_SPAN
    col_ids = jnp.arange(nblocks, dtype=jnp.int32)
    int_score = jax.random.randint(jax.random.fold_in(key, 201), (CHANNEL_TOTAL, nblocks), 0, 1 << 20, dtype=jnp.int32) * nblocks + col_ids[None, :]
    return lax.top_k(int_score, GLOBALS)[1].astype(jnp.int32)


def draw_anchor_tiles(key, part):
    return pick_globals(key)


def draw_sampled_tiles(key, part):
    nblocks = LENGTH // TILE_SPAN
    glob_list = pick_globals(key)
    row_ids = jnp.arange(nblocks, dtype=jnp.int32)
    col_ids = jnp.arange(nblocks, dtype=jnp.int32)
    near_band = jnp.abs(row_ids[:, None] - col_ids[None, :]) <= 1
    is_global = jnp.any(glob_list[:, :, None] == col_ids[None, None, :], axis=1)
    banned = near_band[None, :, :] | is_global[:, None, :]
    int_score = jax.random.randint(jax.random.fold_in(key, 301), (CHANNEL_TOTAL, nblocks, nblocks), 0, 1 << 20, dtype=jnp.int32) * nblocks + col_ids[None, None, :]
    int_score = jnp.where(banned, -1, int_score)
    return lax.top_k(int_score, RANDOM)[1].astype(jnp.int32)


def steps_of(rng, extent, shards, low, high):
    def one(axis_at, parts):
        heights = jax.random.uniform(jax.random.fold_in(jax.random.fold_in(rng, 6), axis_at), (parts,), jnp.float32, low / len(shards), high / len(shards))
        return jnp.repeat(jnp.exp(heights), extent[axis_at] // parts).reshape((-1,) + (1,) * (len(extent) - axis_at - 1))

    factor_of = one(*shards[0])
    for cut in shards[1:]:
        factor_of = factor_of * one(*cut)
    return factor_of


def gaussian(stream_key, dims, deviation, limit, shards=(), kind=jnp.bfloat16):
    loudness = steps_of(stream_key, dims, shards, -0.22, 0.18) if shards else 1.0
    entries = jax.random.normal(stream_key, dims, jnp.float32) * deviation * loudness
    return jnp.minimum(jnp.maximum(entries, -limit), limit).astype(kind)


def setup_inputs(seed: int = 0) -> dict:
    key_of = jax.random.split(jax.random.key(seed), 8)
    return {
        "probe_tensor": draw_probe_tensor(jax.random.fold_in(key_of[7], 71), 0),
        "matcher_tensor": draw_matcher_tensor(jax.random.fold_in(key_of[7], 71), 0),
        "payload_tensor": gaussian(key_of[2], (LENGTH, BATCH, ATT_WIDTH), 1.0, 6.0, ((0, 64), (1, 8))),
        "adjoint_attended": gaussian(key_of[3], (LENGTH, BATCH, ATT_WIDTH), 1.0, 6.0, ((0, 64), (1, 8))),
        "logit_scale": jnp.clip(jnp.exp(jax.random.uniform(key_of[4], (CHANNEL_TOTAL,), jnp.float32, math.log(0.5), math.log(2.0))), 0.5, 2.0),
        "anchor_tiles": draw_anchor_tiles(jax.random.fold_in(key_of[7], 71), 0),
        "sampled_tiles": draw_sampled_tiles(jax.random.fold_in(key_of[7], 71), 0),
    }


masked_minimum = -1e+30

def group_of(count):
    for size in (8, 4, 2):
        if count % size == 0:
            return size
    return 1

def block_lists(anchor_tiles, sampled_tiles, nblocks):
    channel_roster = anchor_tiles.shape[0]
    block_ids = jnp.arange(nblocks, dtype=jnp.int32)
    offsets = jnp.array([-1, 0, 1], dtype=jnp.int32)
    window = jnp.broadcast_to((block_ids[:, None] + offsets[None, :])[None], (channel_roster, nblocks, 3))
    window_ok = (window >= 0) & (window < nblocks)
    glob_slots = jnp.broadcast_to(anchor_tiles[:, None, :], (channel_roster, nblocks, anchor_tiles.shape[1])).astype(jnp.int32)
    glob_ok = jnp.abs(glob_slots - block_ids[None, :, None]) > 1
    rand_ok = jnp.ones(sampled_tiles.shape, dtype=bool)
    position_pointer = jnp.concatenate([window, glob_slots, sampled_tiles.astype(jnp.int32)], axis=2)
    position_pointer = jnp.clip(position_pointer, 0, nblocks - 1).astype(jnp.int32)
    position_usable = jnp.concatenate([window_ok, glob_ok, rand_ok], axis=2)
    return (position_pointer, position_usable)

def share_units(device_portion, tok_local, seq_parts, copies, tile_index, tile_span):
    piece = tok_local // copies
    per_piece = piece // tile_index
    units = jnp.arange(seq_parts * per_piece, dtype=jnp.int32)
    position = units // per_piece * tok_local + device_portion * piece + units % per_piece * tile_index
    return (position // tile_span).astype(jnp.int32)

def attend_sample(probe_vector, matcher_tiles, payload_tiles, adjoint_signal, channel_scale, position_pointer, position_usable, tile_index, tile_span):
    q_len, channel_width = probe_vector.shape
    k_len = matcher_tiles.shape[0]
    q_units = q_len // tile_index
    k_blocks = k_len // tile_span
    group_size = group_of(q_units)
    group_count = q_units // group_size
    reciprocal_sqrt_width = 1.0 / math.sqrt(channel_width)
    key_blocks = matcher_tiles.reshape(k_blocks, tile_span, channel_width).astype(jnp.float32)
    value_blocks = payload_tiles.reshape(k_blocks, tile_span, channel_width).astype(jnp.float32)
    q_groups = probe_vector.reshape(group_count, group_size, tile_index, channel_width).astype(jnp.float32)
    g_groups = adjoint_signal.reshape(group_count, group_size, tile_index, channel_width).astype(jnp.float32)
    i_groups = position_pointer.reshape(group_count, group_size, -1)
    v_groups = position_usable.reshape(group_count, group_size, -1)

    def step(carried, inputs):
        key_acc, value_acc, temp_acc = carried
        q_blk, g_blk, idx_blk, ok_blk = inputs
        k_sel = key_blocks[idx_blk]
        v_sel = value_blocks[idx_blk]
        logit_matrix = jnp.einsum('gbd,gsjd->gbsj', q_blk, k_sel) * reciprocal_sqrt_width
        position_filter = ok_blk[:, None, :, None]
        rescaled_logits = jnp.where(position_filter, channel_scale * logit_matrix, masked_minimum)
        row_max = lax.optimization_barrier(jnp.max(rescaled_logits, axis=(2, 3), keepdims=True))
        expo_terms = jnp.where(position_filter, jnp.exp(rescaled_logits - row_max), 0.0)
        row_total = lax.optimization_barrier(jnp.sum(expo_terms, axis=(2, 3), keepdims=True))
        attn_prob = expo_terms / row_total
        prob_low = attn_prob.astype(jnp.bfloat16).astype(jnp.float32)
        d_prob = jnp.einsum('gbd,gsjd->gbsj', g_blk, v_sel)
        row_delta = lax.optimization_barrier(jnp.sum(attn_prob * d_prob, axis=(2, 3), keepdims=True))
        adjoint_weights = attn_prob * (d_prob - row_delta)
        temp_acc = temp_acc + jnp.sum(adjoint_weights * logit_matrix)
        adjoint_logits = (adjoint_weights * (channel_scale * reciprocal_sqrt_width)).astype(jnp.bfloat16).astype(jnp.float32)
        adjoint_probe = jnp.einsum('gbsj,gsjd->gbd', adjoint_logits, k_sel)
        d_keys = jnp.einsum('gbsj,gbd->gsjd', adjoint_logits, q_blk)
        d_values = jnp.einsum('gbsj,gbd->gsjd', prob_low, g_blk)
        key_acc = key_acc.at[idx_blk].add(d_keys)
        value_acc = value_acc.at[idx_blk].add(d_values)
        return ((key_acc, value_acc, temp_acc), adjoint_probe.astype(jnp.bfloat16))
    start = (jnp.zeros((k_blocks, tile_span, channel_width), jnp.float32), jnp.zeros((k_blocks, tile_span, channel_width), jnp.float32), jnp.zeros((), jnp.float32))
    (key_acc, value_acc, temp_acc), adjoint_probe = lax.scan(step, start, (q_groups, g_groups, i_groups, v_groups))
    return (adjoint_probe.reshape(q_len, channel_width), key_acc.reshape(k_len, channel_width).astype(jnp.bfloat16), value_acc.reshape(k_len, channel_width).astype(jnp.bfloat16), temp_acc)

def reference(probe_tensor, matcher_tensor, payload_tensor, adjoint_attended, logit_scale, anchor_tiles, sampled_tiles):
    length, batch, width = probe_tensor.shape
    channel_roster = logit_scale.shape[0]
    channel_width = width // channel_roster
    nblocks = length // TILE_SPAN
    position_pointer, position_usable = block_lists(anchor_tiles, sampled_tiles, nblocks)
    piece = SEQ_TOK // SHARES
    tile_index = min(TILE_SPAN, piece)

    def to_samples(array):
        return array.reshape(length, batch * channel_roster, channel_width).transpose(1, 0, 2)
    channel_finder = jnp.arange(batch * channel_roster, dtype=jnp.int32) % channel_roster

    def sample_mapped(sample_operands):
        probe_vector, matcher_tiles, payload_tiles, adjoint_signal, channel_ordinal = sample_operands
        channel_scale = logit_scale[channel_ordinal]
        sample_indices = position_pointer[channel_ordinal]
        sample_valid_mask = position_usable[channel_ordinal]
        probe_pieces = probe_vector.reshape(N_SEQ, SHARES, piece, channel_width)
        adjoint_pieces = adjoint_signal.reshape(N_SEQ, SHARES, piece, channel_width)
        query_parts = []
        key_total = jnp.zeros((length, channel_width), jnp.float32)
        value_total = jnp.zeros((length, channel_width), jnp.float32)
        scale_accumulator = jnp.zeros((), jnp.float32)
        for device_portion in range(SHARES):
            tiles_per_device = share_units(device_portion, SEQ_TOK, N_SEQ, SHARES, tile_index, TILE_SPAN)
            adjoint_probe, adjoint_matcher, adjoint_payload, adjoint_scale = attend_sample(probe_pieces[:, device_portion].reshape(-1, channel_width), matcher_tiles, payload_tiles, adjoint_pieces[:, device_portion].reshape(-1, channel_width), channel_scale, sample_indices[tiles_per_device], sample_valid_mask[tiles_per_device], tile_index, TILE_SPAN)
            query_parts.append(adjoint_probe.reshape(N_SEQ, 1, piece, channel_width))
            key_total = key_total + adjoint_matcher.astype(jnp.float32)
            value_total = value_total + adjoint_payload.astype(jnp.float32)
            scale_accumulator = scale_accumulator + adjoint_scale
        return (jnp.concatenate(query_parts, axis=1).reshape(length, channel_width), key_total.astype(jnp.bfloat16), value_total.astype(jnp.bfloat16), scale_accumulator)
    adjoint_probe, adjoint_matcher, adjoint_payload, adjoint_scale = lax.map(sample_mapped, (to_samples(probe_tensor), to_samples(matcher_tensor), to_samples(payload_tensor), to_samples(adjoint_attended), channel_finder))

    def to_flat_sequence(array):
        return array.transpose(1, 0, 2).reshape(length, batch, width)
    adjoint_scales = jax.ops.segment_sum(adjoint_scale, channel_finder, num_segments=channel_roster)
    return (to_flat_sequence(adjoint_probe), to_flat_sequence(adjoint_matcher), to_flat_sequence(adjoint_payload), adjoint_scales)
```

```python
import math

import jax
import jax.numpy as jnp
from jax import lax
from jax.experimental import pallas as pl
from jax.experimental.pallas import tpu as pltpu
from jax.sharding import Mesh, PartitionSpec as P

TILE = 64
WIDTH = 128
SLOTS = 8
NY = 4
TAIL = 8
MASKED = -1e30
LOG2E = 1.4426950408889634


def attend_kernel(
    y_ref, row_ref, scale_ref, bias_ref, qg_ref, own_ref, left_ref, right_ref, far0_ref, far1_ref,
    dq_ref, pown_ref, pleft_ref, pright_ref, pfar0_ref, pfar1_ref,
    kv, acc, temp, sems,
):
    pairs = qg_ref.shape[0] // (4 * TILE)
    shard = kv.shape[0] // NY
    half = shard // 2
    y_at = y_ref[0]

    def start_of(step):
        return pl.multiple_of(lax.rem(y_at + step, NY) * shard, shard)

    places = (
        (own_ref, pown_ref, start_of(0), shard),
        (left_ref, pleft_ref, start_of(3), shard),
        (right_ref, pright_ref, start_of(1), shard),
        (far0_ref, pfar0_ref, start_of(2), half),
        (far1_ref, pfar1_ref, start_of(2) + half, half),
    )
    copies = [
        pltpu.make_async_copy(source, kv.at[pl.ds(start, size), :], sems.at[n])
        for n, (source, _, start, size) in enumerate(places)
    ]
    for copy in copies:
        copy.start()

    def clear(n, carry):
        acc[pl.ds(pl.multiple_of(n * 256, 256), 256), :] = jnp.zeros((256, WIDTH), jnp.float32)
        return carry

    lax.fori_loop(0, acc.shape[0] // 256, clear, 0)
    temp[...] = jnp.zeros_like(temp)
    for copy in copies:
        copy.wait()

    inv = 1.0 / math.sqrt(WIDTH)
    coef = scale_ref[0] * inv
    coef2 = coef * LOG2E
    low_half = lax.broadcasted_iota(jnp.int32, (2 * TILE, WIDTH), 0) < TILE

    def split(x):
        zero = jnp.zeros_like(x)
        return jnp.concatenate(
            [jnp.where(low_half, x, zero), jnp.where(low_half, zero, x)], axis=1
        )

    def pair_step(p, carry):
        base = pl.multiple_of(p * 4 * TILE, 4 * TILE)
        q_diag = split(qg_ref[pl.ds(base, 2 * TILE), :])
        g_diag = split(qg_ref[pl.ds(base + 2 * TILE, 2 * TILE), :])
        at_a = [pl.multiple_of(row_ref[p * 2 * SLOTS + s], TILE) for s in range(SLOTS)]
        at_b = [pl.multiple_of(row_ref[p * 2 * SLOTS + SLOTS + s], TILE) for s in range(SLOTS)]

        def gather(shift):
            return jnp.concatenate(
                [
                    jnp.concatenate(
                        [
                            kv[pl.ds(at_a[s] + shift, TILE), :],
                            kv[pl.ds(at_b[s] + shift, TILE), :],
                        ],
                        axis=1,
                    )
                    for s in range(SLOTS)
                ],
                axis=0,
            )

        k_cat = gather(0)
        v_cat = gather(2 * TILE)
        nt = (((1,), (1,)), ((), ()))
        nn = (((1,), (0,)), ((), ()))
        tn = (((0,), (0,)), ((), ()))
        raw = lax.dot_general(k_cat, q_diag, nt, preferred_element_type=jnp.float32)
        bias = jnp.concatenate(
            [
                jnp.broadcast_to(bias_ref[p, s : s + 1, :], (TILE, 2 * TILE))
                for s in range(SLOTS)
            ],
            axis=0,
        )
        logits = raw * coef2 + bias
        top = jnp.max(logits, axis=0, keepdims=True)
        expo = jnp.exp2(logits - top)
        prob = expo * (1.0 / jnp.sum(expo, axis=0, keepdims=True))
        dprob = lax.dot_general(v_cat, g_diag, nt, preferred_element_type=jnp.float32)
        delta = jnp.sum(prob * dprob, axis=0, keepdims=True)
        dscore = prob * (dprob - delta)
        prod = dscore * raw
        temp[...] += jnp.sum(prod.reshape(SLOTS * TILE // 8, 8, 2 * TILE), axis=0)
        draw = (dscore * coef).astype(jnp.bfloat16)
        prob_low = prob.astype(jnp.bfloat16)
        dk_cat = lax.dot_general(draw, q_diag, nn, preferred_element_type=jnp.float32)
        dv_cat = lax.dot_general(prob_low, g_diag, nn, preferred_element_type=jnp.float32)
        for s in range(SLOTS):
            rows = slice(s * TILE, (s + 1) * TILE)
            for at, cols in ((at_a[s], slice(0, WIDTH)), (at_b[s], slice(WIDTH, 2 * WIDTH))):
                acc[pl.ds(at, TILE), :] += dk_cat[rows, cols]
                acc[pl.ds(at + 2 * TILE, TILE), :] += dv_cat[rows, cols]
        dq_cat = lax.dot_general(draw, k_cat, tn, preferred_element_type=jnp.float32)
        dq_ref[p, : 2 * TILE, :] = jnp.where(
            low_half, dq_cat[:, :WIDTH], dq_cat[:, WIDTH:]
        ).astype(jnp.bfloat16)
        return carry

    lax.fori_loop(0, pairs, pair_step, 0)

    total = jnp.sum(temp[...], keepdims=True) * inv
    high = total.astype(jnp.bfloat16).astype(jnp.float32)
    mid = (total - high).astype(jnp.bfloat16).astype(jnp.float32)
    low = total - high - mid
    line = lax.broadcasted_iota(jnp.int32, (TAIL, WIDTH), 0)
    tail = jnp.where(line == 0, high, jnp.where(line == 1, mid, low)).astype(jnp.bfloat16)
    for p in range(pairs):
        dq_ref[p, 2 * TILE :, :] = tail

    for _, target, start, size in places:
        def narrow(n, carry, target=target, start=start):
            at = pl.multiple_of(n * 256, 256)
            target[pl.ds(at, 256), :] = acc[pl.ds(start + at, 256), :].astype(jnp.bfloat16)
            return carry

        lax.fori_loop(0, size // 256, narrow, 0)


def local_attend(y_at, index, usable, scale, qg, own, left, right, far0, far1):
    count = index.shape[0]
    bias = jnp.where(usable, 0.0, MASKED).astype(jnp.float32)
    bias = bias.reshape(count // 2, 2, SLOTS).transpose(0, 2, 1)
    bias = jnp.repeat(bias, TILE, axis=2)
    rows = index // 2 * (4 * TILE) + index % 2 * TILE
    pairs, shard = count // 2, own.shape[0]
    vmem = pl.BlockSpec(memory_space=pltpu.VMEM)
    smem = pl.BlockSpec(memory_space=pltpu.SMEM)
    hbm = pl.BlockSpec(memory_space=pl.ANY)
    part = jax.ShapeDtypeStruct((shard, WIDTH), jnp.bfloat16)
    half = jax.ShapeDtypeStruct((shard // 2, WIDTH), jnp.bfloat16)
    return pl.pallas_call(
        attend_kernel,
        out_shape=(
            jax.ShapeDtypeStruct((pairs, 2 * TILE + TAIL, WIDTH), jnp.bfloat16),
            part, part, part, half, half,
        ),
        in_specs=[smem, smem, smem, vmem, vmem, hbm, hbm, hbm, hbm, hbm],
        out_specs=(vmem,) * 6,
        scratch_shapes=[
            pltpu.VMEM((NY * shard, WIDTH), jnp.bfloat16),
            pltpu.VMEM((NY * shard, WIDTH), jnp.float32),
            pltpu.VMEM((8, WIDTH), jnp.float32),
            pltpu.SemaphoreType.DMA((5,)),
        ],
        compiler_params=pltpu.CompilerParams(vmem_limit_bytes=48 * 1024 * 1024),
        name="attend",
    )(
        y_at.reshape(1).astype(jnp.int32), rows.reshape(-1), scale, bias, qg,
        own, left, right, far0, far1,
    )


def slot_lists(anchor_tiles, sampled_tiles, head, first, count, nblocks):
    block = first + jnp.arange(count, dtype=jnp.int32)
    window = block[:, None] + jnp.array([-1, 0, 1], dtype=jnp.int32)[None, :]
    anchors = lax.dynamic_index_in_dim(anchor_tiles, head, 0, keepdims=True)
    anchors = jnp.broadcast_to(anchors, (count, anchors.shape[1]))
    sampled = lax.dynamic_slice(
        sampled_tiles, (head, first, 0), (1, count, sampled_tiles.shape[2])
    )[0]
    index = jnp.concatenate([window, anchors, sampled], axis=1)
    usable = jnp.concatenate(
        [
            (window >= 0) & (window < nblocks),
            jnp.abs(anchors - block[:, None]) > 1,
            jnp.ones(sampled.shape, dtype=bool),
        ],
        axis=1,
    )
    return jnp.clip(index, 0, nblocks - 1), usable


def on_device(probe, matcher, payload, adjoint, logit_scale, anchor_tiles, sampled_tiles):
    tok_local, seq_count, width = probe.shape
    heads = logit_scale.shape[0]
    n_fsdp = lax.axis_size("fsdp")
    y_at, z_at = lax.axis_index("y"), lax.axis_index("z")

    def by_head(array):
        return array.reshape(tok_local, heads, WIDTH).transpose(1, 0, 2)

    def to_head(first, second):
        both = jnp.stack([by_head(first), by_head(second)], axis=1)
        return lax.all_to_all(both, "z", split_axis=0, concat_axis=0, tiled=True)

    def to_tokens(array):
        return array.transpose(1, 0, 2).reshape(tok_local, seq_count, width)

    def shift(array, step):
        return lax.ppermute(array, "y", [(n, (n + step) % NY) for n in range(NY)])

    own = to_head(matcher, payload)
    shard = own.size // WIDTH
    own = own.reshape(shard, WIDTH)
    half = shard // 2
    left = shift(own, 1)
    right = shift(own, -1)
    far0 = shift(left[:half], 1)
    far1 = shift(right[half:], -1)
    qg = to_head(probe, adjoint).reshape(shard, WIDTH)

    nblocks = NY * heads * tok_local // TILE
    count = nblocks // NY
    index, usable = slot_lists(
        anchor_tiles, sampled_tiles, z_at, y_at * count, count, nblocks
    )
    scale = lax.dynamic_slice(logit_scale, (z_at,), (1,))
    dq, pown, pleft, pright, pfar0, pfar1 = local_attend(
        y_at, index, usable, scale, qg, own, left, right, far0, far1
    )

    def add(*parts):
        total = parts[0].astype(jnp.float32)
        for other in parts[1:]:
            total = total + other.astype(jnp.float32)
        return total.astype(jnp.bfloat16)

    dq = lax.all_to_all(dq, "z", split_axis=0, concat_axis=0, tiled=True)
    from_left = shift(pfar0, 1)
    from_right = shift(pfar1, -1)
    right_sum = jnp.concatenate([add(pright[:half], from_left), pright[half:]], axis=0)
    left_sum = jnp.concatenate([pleft[:half], add(pleft[half:], from_right)], axis=0)
    mine = add(pown, shift(right_sum, 1), shift(left_sum, -1))
    mine = lax.all_to_all(
        mine.reshape(heads, 2, tok_local, WIDTH), "z", split_axis=0, concat_axis=0, tiled=True
    )

    temp = jnp.sum(dq[:, tok_local : tok_local + 3, 0].astype(jnp.float32), axis=1)
    for bit in range(n_fsdp.bit_length() - 1):
        swap = [(n, n ^ (1 << bit)) for n in range(n_fsdp)]
        temp = temp + lax.ppermute(temp, "fsdp", swap)
    for bit in range(NY.bit_length() - 1):
        swap = [(n, n ^ (1 << bit)) for n in range(NY)]
        temp = temp + lax.ppermute(temp, "y", swap)

    return to_tokens(dq[:, :tok_local]), to_tokens(mine[:, 0]), to_tokens(mine[:, 1]), temp


def solution(mesh):
    seq, fsdp = mesh.shape["seq"], mesh.shape["fsdp"]
    split_mesh = Mesh(mesh.devices.reshape(NY, seq // NY, fsdp), ("y", "z", "fsdp"))
    tokens = P(("y", "z"), "fsdp", None)
    return jax.shard_map(
        on_device,
        mesh=split_mesh,
        in_specs=(tokens, tokens, tokens, tokens, P(), P(), P()),
        out_specs=(tokens, tokens, tokens, P()),
        check_vma=False,
    )
```
